32 devices in a mesh: dp: 8 (over z, y), sub: 4 (over x, core).
Axes of the slice: x: 2, y: 2, z: 4, core: 2. Of those that a mesh axis runs over, the one named last changes fastest.
Arguments:
- vectors: bfloat16 [16384, 1024], P(('dp', 'sub'))
- assignments: int32 [16384, 64], P('dp', 'sub'), may hold values from 0 to 255, as said below
- codebooks: float32 [64, 16, 256], replicated
Outputs:
- rotated: bfloat16 [16384, 1024], P('dp', 'sub')
- new_books: float32 [64, 16, 256], P('sub')
The draws below stay inside these ranges and needn't reach their ends.
Inputs may be any that keep to these rules, and one draw needn't show every extreme that they name: `assignments`: in subspaces of odd index every code is below K - K // 16; in subspaces of even index every code 0 to K - 1 occurs.
All inputs are finite; a program needn't handle non-finite values.
Results may differ from the reference program's by a relative error of at most 0.0044.
Values may be sent and summed in bfloat16 or wider, within the bound.
A program may use at most 64 MiB of HBM per device.

```python
import math
import jax
import jax.numpy as jnp
from jax import lax

D = 1024
M = 64
K = 256
DS = 16
ROWS_DEV = 512
NS_ITERS = 2
TOTAL_ROWS = 16384


def opq_sample(key):
    base = jax.random.fold_in(key, 7)
    keys = jax.random.split(base, 10)
    row_ids = jnp.arange(TOTAL_ROWS, dtype=jnp.int32)[:, None]
    sub_ids = jnp.arange(M, dtype=jnp.int32)[None, :]
    raw_even = jax.random.randint(keys[0], (TOTAL_ROWS, M), 0, K)
    raw_odd = jax.random.randint(keys[1], (TOTAL_ROWS, M), 0, K - K // 16)
    shuffled = jax.random.permutation(keys[2], K)
    forced = shuffled[jnp.clip(row_ids, 0, K - 1)]
    even_codes = jnp.where(row_ids < K, forced, raw_even)
    codes = jnp.where(sub_ids % 2 == 1, raw_odd, even_codes).astype(jnp.int32)
    book_scale = jnp.exp(math.log(4.0) * jax.random.uniform(keys[3], (M, DS, 1)))
    book_base = jax.random.normal(keys[4], (M, DS, K))
    books = 0.6 * book_base * book_scale
    books_t = jnp.transpose(books, (0, 2, 1))
    rebuilt = books_t[jnp.arange(M)[None, :], codes].reshape(TOTAL_ROWS, D)
    block_total = TOTAL_ROWS // ROWS_DEV
    multipliers = 2 * jax.random.randint(keys[5], (block_total,), 0, D // 2) + 1
    offsets = jax.random.randint(keys[6], (block_total,), 0, D)
    signs = (2 * jax.random.randint(keys[7], (block_total, 1, D), 0, 2) - 1).astype(jnp.float32)
    targets = (multipliers[:, None] * jnp.arange(D, dtype=jnp.int32)[None, :] + offsets[:, None]) % D
    blocked = rebuilt.reshape(block_total, ROWS_DEV, D)
    mixed = jax.vmap(lambda values, where_to: values[:, where_to])(blocked, targets)
    mixed = (signs * mixed).reshape(TOTAL_ROWS, D)
    column_pos = jnp.arange(D, dtype=jnp.float32)[None, :] / D
    column_scale = 0.3 * jnp.exp(math.log(10.0) * column_pos + 0.7 * (jax.random.uniform(keys[8], (1, D)) - 0.5))
    row_pos = jnp.arange(TOTAL_ROWS, dtype=jnp.float32)[:, None] / TOTAL_ROWS
    noise = jax.random.normal(keys[9], (TOTAL_ROWS, D))
    row_scale = 0.6 + 1.2 * row_pos
    vectors = row_scale * column_scale * (0.7 * rebuilt + 0.5 * mixed + 0.5 * noise)
    return (codes, books, vectors)


def draw_vectors(key, part):
    return opq_sample(key)[2].astype(jnp.bfloat16)


def draw_assignments(key, part):
    return opq_sample(key)[0]


def draw_codebooks(key, part):
    return opq_sample(key)[1].astype(jnp.float32)


def setup_inputs(seed: int = 0) -> dict:
    key_list = jax.random.split(jax.random.key(seed), 4)
    return {
        "vectors": draw_vectors(jax.random.fold_in(key_list[3], 71), 0),
        "assignments": draw_assignments(jax.random.fold_in(key_list[3], 71), 0),
        "codebooks": draw_codebooks(jax.random.fold_in(key_list[3], 71), 0),
    }


def rebuild(block_codes, low_books):
    books_t = jnp.transpose(low_books, (0, 2, 1))
    picked = books_t[jnp.arange(M)[None, :], block_codes]
    return picked.reshape(block_codes.shape[0], D)

def reference(vectors, assignments, codebooks):
    low_books = codebooks.astype(jnp.bfloat16)
    block_total = TOTAL_ROWS // ROWS_DEV
    vec_blocks = vectors.reshape(block_total, ROWS_DEV, D)
    code_blocks = assignments.reshape(block_total, ROWS_DEV, M)

    def accumulate(carry, paired):
        block_vec, block_code = paired
        rebuilt = rebuild(block_code, low_books)
        term = lax.dot_general(block_vec, rebuilt, (((0,), (0,)), ((), ())), preferred_element_type=jnp.float32)
        return (carry + term, None)
    covariance, unused = lax.scan(accumulate, jnp.zeros((D, D), jnp.float32), (vec_blocks, code_blocks))
    iterate = covariance * (math.sqrt(D) / 3.0) / jnp.sqrt(jnp.sum(covariance * covariance))
    for sweep in range(NS_ITERS):
        gram = jnp.dot(iterate.T, iterate, precision=lax.Precision.HIGHEST, preferred_element_type=jnp.float32)
        iterate = 1.5 * iterate - 0.5 * jnp.dot(iterate, gram, precision=lax.Precision.HIGHEST, preferred_element_type=jnp.float32)
    rotation = iterate.astype(jnp.bfloat16)
    rotated = jnp.dot(vectors, rotation, preferred_element_type=jnp.float32).astype(jnp.bfloat16)
    levels = jnp.arange(K, dtype=jnp.int32)

    def per_subspace(subspace):
        column_block = lax.dynamic_slice_in_dim(rotated, subspace * DS, DS, 1)
        code_column = lax.dynamic_slice_in_dim(assignments, subspace, 1, 1)
        onehot = (code_column == levels[None, :]).astype(jnp.bfloat16)
        code_sums = lax.dot_general(column_block, onehot, (((0,), (0,)), ((), ())), preferred_element_type=jnp.float32)
        counts = lax.optimization_barrier(jnp.sum(onehot, axis=0, dtype=jnp.float32))
        return (code_sums, counts)
    code_sums, counts = lax.map(per_subspace, jnp.arange(M, dtype=jnp.int32))
    new_books = jnp.where(counts[:, None, :] > 0, code_sums / jnp.maximum(counts, 1.0)[:, None, :], codebooks)
    return (rotated, new_books)
```

```python
import functools
import math

import jax
import jax.numpy as jnp
from jax import lax
from jax.experimental import pallas as pl
from jax.experimental.pallas import tpu as pltpu
from jax.sharding import PartitionSpec as P

NS_ITERS = 2
MESH = pl.DeviceIdType.MESH
F32, BF16 = jnp.float32, jnp.bfloat16
NN = (((1,), (0,)), ((), ()))
NT = (((1,), (1,)), ((), ()))


def dot(a, b, dims=NN):
    return lax.dot_general(a, b, dims, preferred_element_type=F32)


def split_dot(a, b, dims=NN, passes=1):
    high = a.astype(BF16)
    out = dot(high, b, dims)
    if passes == 2:
        out = out + dot((a - high.astype(F32)).astype(BF16), b, dims)
    return out


def kernel(
    nd, chunks, passes,
    vec_ref, asg_ref, books_ref, rotated_ref, new_books_ref,
    gv, oh, rt, cpart, rsin, ct, cnt, cntin, sums, sumsin, means, zt, rott,
    own_sem, v_send, v_recv, n_send, n_recv, r_send, r_recv, a_send, a_recv,
    g_send, g_recv, s_send, s_recv, m_send, m_recv,
):
    d, s = lax.axis_index("dp"), lax.axis_index("sub")
    mate = s + 1 - 2 * (s % 2)
    across = (s + 2) % 4
    rows, feats = vec_ref.shape
    own_subs, total_rows = asg_ref.shape
    width, levels = books_ref.shape[1], books_ref.shape[2]
    cols = own_subs * width
    cw = feats // chunks
    row_groups = min(nd, 16)
    col_groups = nd // row_groups
    ph, pw = cols // row_groups, cw // col_groups
    sh = cols // nd

    barrier = pltpu.get_barrier_semaphore()
    for k in range(1, nd):
        pl.semaphore_signal(barrier, inc=1, device_id=((d + k) % nd, s), device_id_type=MESH)
    for peer in (mate, across):
        pl.semaphore_signal(barrier, inc=1, device_id=(d, peer), device_id_type=MESH)
    pl.semaphore_wait(barrier, nd + 1)

    pending = []

    def send(src, dst, send_sem, recv_sem, target):
        copy = pltpu.make_async_remote_copy(
            src_ref=src, dst_ref=dst, send_sem=send_sem, recv_sem=recv_sem,
            device_id=target, device_id_type=MESH,
        )
        copy.start()
        pending.append(copy)
        return copy

    def span(block, size):
        return pl.ds(pl.multiple_of(block * size, size), size)

    def strip(c):
        return pl.ds(c * cw, cw)

    own_rows = span(s, rows)
    own_copy = pltpu.make_async_copy(vec_ref, gv.at[own_rows], own_sem)
    own_copy.start()
    v_across, v_mate, v_pass = [], [], []
    for c in range(chunks):
        src = vec_ref.at[:, strip(c)]
        dst = gv.at[own_rows, strip(c)]
        v_across.append(send(src, dst, v_send.at[0, c], v_recv.at[0, c], (d, across)))
        v_mate.append(send(src, dst, v_send.at[1, c], v_recv.at[1, c], (d, mate)))

    def pass_vectors(c):
        v_across[c].wait_recv()
        block = gv.at[span(across, rows), strip(c)]
        v_pass.append(send(block, block, v_send.at[2, c], v_recv.at[2, c], (d, mate)))

    level = lax.broadcasted_iota(jnp.int32, (levels, 512), 0)
    ones = jnp.ones((16, total_rows), BF16)

    def build(m, carry):
        for b in range(total_rows // 512):
            code = asg_ref[pl.ds(m, 1), pl.ds(b * 512, 512)]
            oh[m, :, pl.ds(b * 512, 512)] = jnp.where(level == code, 1.0, 0.0).astype(BF16)
        book = books_ref[s * own_subs + m].astype(BF16)
        rt[span(m, width), :] = dot(book, oh[m]).astype(BF16)
        cnt[pl.ds(m, 1), :] = dot(ones, oh[m], NT)[0:1]
        return carry

    parts = 4
    for part in range(parts):
        step = own_subs // parts
        lax.fori_loop(part * step, (part + 1) * step, build, 0)
        if part % 2 == 1:
            pass_vectors(part // 2)
    n_copies = [
        send(cnt, cntin.at[k - 1], n_send.at[k - 1], n_recv.at[k - 1], ((d + k) % nd, s))
        for k in range(1, nd)
    ]
    own_copy.wait()

    def piece(q, c):
        r = pl.ds(pl.multiple_of((q % row_groups) * ph, ph), ph)
        w = pl.ds(pl.multiple_of(c * cw + (q // row_groups) * pw, pw), pw)
        return r, w

    def global_piece(q, c):
        r = pl.ds(pl.multiple_of(s * cols + (q % row_groups) * ph, ph), ph)
        return r, piece(q, c)[1]

    r_copies, a_copies, g_across, g_mate, g_pass = {}, {}, {}, {}, {}
    for t in range(chunks + 3):
        if t < chunks:
            for c in range(chunks):
                if c == len(v_pass) and c <= t + 1:
                    pass_vectors(c)
            v_mate[t].wait_recv()
            v_pass[t].wait_recv()
            cpart[:, strip(t)] = dot(rt[...], gv[:, strip(t)])
            for k in range(1, nd):
                q = (d + k) % nd
                r_copies[t, k] = send(
                    cpart.at[piece(q, t)], rsin.at[t, k - 1],
                    r_send.at[t, k - 1], r_recv.at[t, k - 1], (q, s),
                )
        c = t - 1
        if 0 <= c < chunks:
            total = cpart[piece(d, c)]
            for k in range(1, nd):
                r_copies[c, k].wait_recv()
                total = total + rsin[c, k - 1]
            ct[global_piece(d, c)] = total.astype(BF16)
            for k in range(1, nd):
                block = ct.at[global_piece(d, c)]
                a_copies[c, k] = send(
                    block, block, a_send.at[c, k - 1], a_recv.at[c, k - 1], ((d + k) % nd, s)
                )
        c = t - 2
        if 0 <= c < chunks:
            for k in range(1, nd):
                a_copies[c, k].wait_recv()
            block = ct.at[span(s, cols), strip(c)]
            g_across[c] = send(block, block, g_send.at[0, c], g_recv.at[0, c], (d, across))
            g_mate[c] = send(block, block, g_send.at[1, c], g_recv.at[1, c], (d, mate))
        c = t - 3
        if 0 <= c < chunks:
            g_across[c].wait_recv()
            block = ct.at[span(across, cols), strip(c)]
            g_pass[c] = send(block, block, g_send.at[2, c], g_recv.at[2, c], (d, mate))
    for c in range(chunks):
        g_mate[c].wait_recv()
        g_pass[c].wait_recv()

    square = jnp.zeros((8, feats), F32)
    for b in range(feats // 64):
        v = ct[pl.ds(b * 64, 64), :].astype(F32)
        square = square + jnp.sum((v * v).reshape(8, 8, feats), axis=0)
    norm = jnp.sum(square)
    scale = (math.sqrt(feats) / 3.0) / jnp.sqrt(jnp.full((1, feats), norm, F32))
    scale2 = scale * scale

    own = ct[span(s, cols), :]
    gram = dot(own, ct[...], NT) * scale2
    first = 1.5 * own.astype(F32) - 0.5 * split_dot(gram, ct[...], NN, passes)
    half = split_dot(first, ct[...], NT, passes) * scale2
    tail = split_dot(half, ct[...], NN, passes)
    gram1 = 1.5 * half - 0.5 * (split_dot(tail, ct[...], NT, passes) * scale2)
    prod = split_dot(gram1, ct[...], NN, passes)
    back = split_dot(prod, ct[...], NT, passes) * scale2
    second = 1.5 * first - 0.5 * (1.5 * prod - 0.5 * split_dot(back, ct[...], NN, passes))
    zt[...] = (second * scale).astype(BF16)

    for b in range(total_rows // 512):
        block = gv[pl.ds(b * 512, 512), :]
        rott[:, pl.ds(b * 512, 512)] = dot(zt[...], block, NT).astype(BF16)

    def accumulate(m, carry):
        sums[span(m, width), :] = dot(rott[span(m, width), :], oh[m], NT)
        return carry

    lax.fori_loop(0, own_subs, accumulate, 0)
    s_copies = []
    for k in range(1, nd):
        q = (d + k) % nd
        s_copies.append(
            send(sums.at[span(q, sh)], sumsin.at[k - 1], s_send.at[k - 1], s_recv.at[k - 1], (q, s))
        )
    for b in range(total_rows // 512):
        block = gv[pl.ds(b * 512, 512), :]
        rotated_ref[pl.ds(b * 512, 512), :] = dot(block, zt[...], NT).astype(BF16)
    counts = cnt[...]
    for k in range(1, nd):
        n_copies[k - 1].wait_recv()
        counts = counts + cntin[k - 1]
    total = sums[span(d, sh)]
    for k in range(1, nd):
        s_copies[k - 1].wait_recv()
        total = total + sumsin[k - 1]
    means[span(d, sh)] = total
    m_copies = []
    for k in range(1, nd):
        block = means.at[span(d, sh)]
        m_copies.append(
            send(block, block, m_send.at[k - 1], m_recv.at[k - 1], ((d + k) % nd, s))
        )
    for copy in m_copies:
        copy.wait_recv()
    for m in range(own_subs):
        n = counts[m:m + 1]
        value = means[pl.ds(m * width, width), :] / jnp.maximum(n, 1.0)
        new_books_ref[m] = jnp.where(n > 0, value, books_ref[s * own_subs + m])
    for copy in pending:
        copy.wait_send()


def on_device(nd, vectors, assignments, codebooks):
    rows, feats = vectors.shape
    total_rows, own_subs = assignments.shape
    width, levels = codebooks.shape[1:]
    cols = own_subs * width
    chunks = 4
    row_groups = min(nd, 16)
    ph, pw = cols // row_groups, feats // chunks // (nd // row_groups)
    sh = cols // nd
    dma = pltpu.SemaphoreType.DMA
    peers = nd - 1
    vmem = pl.BlockSpec(memory_space=pltpu.VMEM)
    return pl.pallas_call(
        functools.partial(kernel, nd, chunks, 1),
        out_shape=(
            jax.ShapeDtypeStruct((total_rows, cols), BF16),
            jax.ShapeDtypeStruct((own_subs, width, levels), F32),
        ),
        in_specs=[vmem] * 3,
        out_specs=(vmem, vmem),
        scratch_shapes=[
            pltpu.VMEM((total_rows, feats), BF16),
            pltpu.VMEM((own_subs, levels, total_rows), BF16),
            pltpu.VMEM((cols, total_rows), BF16),
            pltpu.VMEM((cols, feats), F32),
            pltpu.VMEM((chunks, peers, ph, pw), F32),
            pltpu.VMEM((feats, feats), BF16),
            pltpu.VMEM((own_subs, levels), F32),
            pltpu.VMEM((peers, own_subs, levels), F32),
            pltpu.VMEM((cols, levels), F32),
            pltpu.VMEM((peers, sh, levels), F32),
            pltpu.VMEM((cols, levels), F32),
            pltpu.VMEM((cols, feats), BF16),
            pltpu.VMEM((cols, total_rows), BF16),
            dma,
            dma((3, chunks)), dma((3, chunks)),
            dma((peers,)), dma((peers,)),
            dma((chunks, peers)), dma((chunks, peers)),
            dma((chunks, peers)), dma((chunks, peers)),
            dma((3, chunks)), dma((3, chunks)),
            dma((peers,)), dma((peers,)),
            dma((peers,)), dma((peers,)),
        ],
        compiler_params=pltpu.CompilerParams(
            collective_id=0, has_side_effects=True, vmem_limit_bytes=58 * 1024 * 1024
        ),
    )(vectors, assignments.T, codebooks)


def solution(mesh):
    in_specs = (P(("dp", "sub"), None), P("dp", "sub"), P())
    out_specs = (P("dp", "sub"), P("sub", None, None))
    return jax.shard_map(
        functools.partial(on_device, mesh.shape["dp"]),
        mesh=mesh, in_specs=in_specs, out_specs=out_specs, check_vma=False,
    )
```
